32 devices in a mesh: dp: 32 (over z, y, x, core), tensor: 1.
Axes of the slice: x: 2, y: 2, z: 4, core: 2. Of those that a mesh axis runs over, the one named last changes fastest.
Arguments:
- tokens: bfloat16 [8192, 2048], P('dp', 'tensor'), may hold values from -6 to 6
- expert_ids: int32 [8192, 2], P('dp'), may hold values from 0 to 31, as said below
- route_weights: float32 [8192, 2], P('dp'), may hold values from 0.2 to 1
- gate_weight: bfloat16 [32, 2048, 1024], P('dp', None, 'tensor'), may hold values from -0.125 to 0.125
- up_weight: bfloat16 [32, 2048, 1024], P('dp', None, 'tensor'), may hold values from -0.125 to 0.125
- down_weight: bfloat16 [32, 1024, 2048], P('dp', 'tensor'), may hold values from -0.1875 to 0.1875
Outputs:
- moe_out: bfloat16 [8192, 2048], P('dp', 'tensor')
The draws below stay inside these ranges and needn't reach their ends.
Inputs may be any that keep to these rules, and one draw needn't show every extreme that they name: `expert_ids`: the two experts of a row differ. Among the rows of one index of dp, no expert is named more than 32 times.
All inputs are finite; a program needn't handle non-finite values.
Results may differ from the reference program's by a relative error of at most 0.011.
Values may be sent and summed in bfloat16 or wider, within the bound.
No kernel may reach another device: no remote copies, remote signals or barrier semaphores. Data moves between devices by JAX's collectives and lax.ppermute only.
A program may use at most 64 MiB of HBM per device.

```python
import jax
import jax.numpy as jnp
from jax import lax

D = 2048
FF = 1024
TOP = 2
TOK_DEV = 256
EXPERTS = 32
TOKENS = 8192
CAP = 32
N_DP = 32
N_TENSOR = 1


def draw_expert_ids(key, part):
    blocks = TOKENS // TOK_DEV
    key_weight, key_hot, key_noise, key_count, key_shuffle = jax.random.split(key, 5)
    popularity = jax.random.randint(key_weight, (EXPERTS,), 1, 9)
    hot_expert = jax.random.randint(key_hot, (), 0, EXPERTS)
    numbers = jnp.arange(EXPERTS, dtype=jnp.int32)
    noise_draw = jax.random.randint(key_noise, (blocks, EXPERTS), 0, 1 << 16)
    scores = noise_draw * popularity[None, :] * EXPERTS + numbers[None, :]
    scores = jnp.where(numbers[None, :] == hot_expert, 1 << 30, scores)
    unused_values, ranked = lax.top_k(scores, EXPERTS)
    least_count = (2 * TOK_DEV - CAP + EXPERTS - 2) // (EXPERTS - 1)
    run_counts = jax.random.randint(key_count, (blocks, EXPERTS), least_count, CAP + 1)
    run_counts = run_counts.at[:, 0].set(CAP)
    run_ends = jnp.cumsum(run_counts, axis=1)
    slot_numbers = jnp.arange(2 * TOK_DEV, dtype=jnp.int32)
    run_index = jnp.sum((slot_numbers[None, :, None] >= run_ends[:, None, :]).astype(jnp.int32), axis=2)
    named = jnp.take_along_axis(ranked, run_index, axis=1)
    paired = jnp.stack([named[:, :TOK_DEV], named[:, TOK_DEV:]], axis=2)
    shuffle_keys = jax.random.split(key_shuffle, blocks)
    shuffled = jax.vmap(lambda one_key: jax.random.permutation(one_key, TOK_DEV))(shuffle_keys)
    paired = jnp.take_along_axis(paired, shuffled[:, :, None], axis=1)
    return paired.reshape(TOKENS, 2).astype(jnp.int32)


def levels(own_key, extent, shards, low, largest):
    def one(dim, parts):
        heights = jax.random.uniform(jax.random.fold_in(jax.random.fold_in(own_key, 6), dim), (parts,), jnp.float32, low / len(shards), largest / len(shards))
        return jnp.repeat(jnp.exp(heights), extent[dim] // parts).reshape((-1,) + (1,) * (len(extent) - dim - 1))

    factor_of = one(*shards[0])
    for cut in shards[1:]:
        factor_of = factor_of * one(*cut)
    return factor_of


def normal_values(rng, extent, deviation, most, cuts=(), kind=jnp.bfloat16):
    entries = deviation * jax.random.normal(rng, extent, jnp.float32)
    if cuts:
        entries = entries * levels(rng, extent, cuts, -0.22, 0.18)
    return jnp.clip(entries, -most, most).astype(kind)


def setup_inputs(seed: int = 0) -> dict:
    seeds = jax.random.split(jax.random.key(seed), 7)
    return {
        "tokens": normal_values(seeds[0], (TOKENS, D), 1.0, 6.0, ((0, 32),)),
        "expert_ids": draw_expert_ids(jax.random.fold_in(seeds[6], 71), 0),
        "route_weights": jnp.clip(0.2 + 0.8 * jax.random.uniform(seeds[2], (TOKENS, TOP), jnp.float32) ** levels(seeds[2], (TOKENS, TOP), ((0, 32),), -0.2, 0.2), 0.2, 1.0),
        "gate_weight": normal_values(seeds[3], (EXPERTS, D, FF), D ** -0.5, 0.125, ((0, 32),)),
        "up_weight": normal_values(seeds[4], (EXPERTS, D, FF), D ** -0.5, 0.125, ((0, 32),)),
        "down_weight": normal_values(seeds[5], (EXPERTS, FF, D), FF ** -0.5, 0.1875, ((0, 32),)),
    }


def reference(tokens, expert_ids, route_weights, gate_weight, up_weight, down_weight):
    chosen = expert_ids.reshape(-1).astype(jnp.int32)
    assignments = chosen.shape[0]
    token_order = jnp.argsort(chosen, stable=True).astype(jnp.int32)
    counts = jax.ops.segment_sum(jnp.ones((assignments,), jnp.int32), chosen, num_segments=EXPERTS).astype(jnp.int32)
    starts = (jnp.cumsum(counts) - counts).astype(jnp.int32)
    most_rows = N_DP * CAP
    padded = jnp.concatenate([token_order, jnp.zeros((most_rows,), jnp.int32)])
    quarter = FF // N_TENSOR

    def expert_out(expert):
        picked = lax.dynamic_slice(padded, (starts[expert].astype(jnp.int32),), (most_rows,))
        token_rows = tokens[picked // 2]
        gate_value = jnp.dot(token_rows, gate_weight[expert], preferred_element_type=jnp.float32)
        up_value = jnp.dot(token_rows, up_weight[expert], preferred_element_type=jnp.float32)
        hidden = (jax.nn.silu(gate_value) * up_value).astype(jnp.bfloat16)
        summed = jnp.zeros((most_rows, D), jnp.float32)
        for share_index in range(N_TENSOR):
            lower = share_index * quarter
            partial_sum = jnp.dot(hidden[:, lower:lower + quarter], down_weight[expert, lower:lower + quarter], preferred_element_type=jnp.float32)
            rounded = lax.optimization_barrier(partial_sum.astype(jnp.bfloat16))
            summed = summed + rounded.astype(jnp.float32)
        return summed.astype(jnp.bfloat16)

    outputs = lax.map(expert_out, jnp.arange(EXPERTS, dtype=jnp.int32))
    position = jnp.zeros((assignments,), jnp.int32).at[token_order].set(jnp.arange(assignments, dtype=jnp.int32))
    rank_in = (position - starts[chosen]).astype(jnp.int32)
    gathered = outputs[chosen, rank_in]
    weighted = gathered.astype(jnp.float32).reshape(-1, TOP, D) * route_weights[:, :, None]
    return jnp.sum(weighted, axis=1).astype(jnp.bfloat16)
```

```python
import functools

import jax
import jax.numpy as jnp
from jax import lax
from jax.experimental import pallas as pl
from jax.experimental.pallas import tpu as pltpu
from jax.sharding import PartitionSpec as P

VMEM_LIMIT = 56 * 1024 * 1024
F32 = jnp.float32
BF16 = jnp.bfloat16


def slot_masks(me, meta, experts, capacity):
    tokens = meta.shape[1]
    names = jnp.bitwise_xor(me, lax.broadcasted_iota(jnp.int32, (experts, tokens), 0)).astype(F32)
    first = meta[0:1, :] == names
    second = meta[1:2, :] == names
    named = jnp.where(first, 1.0, 0.0) + jnp.where(second, 1.0, 0.0)
    weight = jnp.where(first, meta[2:3, :], 0.0) + jnp.where(second, meta[3:4, :], 0.0)
    earlier = jnp.where(
        lax.broadcasted_iota(jnp.int32, (tokens, tokens), 0)
        < lax.broadcasted_iota(jnp.int32, (tokens, tokens), 1),
        1.0,
        0.0,
    )
    rank = jnp.dot(named.astype(BF16), earlier.astype(BF16), preferred_element_type=F32)
    rank = jnp.where(named > 0.5, rank, -1.0).astype(jnp.int32)
    slot = lax.broadcasted_iota(jnp.int32, (experts, capacity, tokens), 1)
    return rank[:, None, :] == slot, weight


def dispatch_kernel(experts, capacity, me_ref, meta_ref, tokens_ref, *outs):
    mask, _ = slot_masks(me_ref[0], meta_ref[...], experts, capacity)
    tokens, width = tokens_ref.shape
    pick = jnp.where(mask, 1.0, 0.0).reshape(experts * capacity, tokens).astype(BF16)
    rows = outs[0].shape[0]
    tile = min(width, 512)
    for col in range(0, width, tile):
        picked = jnp.dot(pick, tokens_ref[:, col : col + tile], preferred_element_type=F32)
        picked = picked.astype(BF16)
        for k, out in enumerate(outs):
            out[:, col : col + tile] = picked[k * rows : (k + 1) * rows]


def dispatch(me, meta, tokens, blocks, capacity):
    width = tokens.shape[1]
    vmem = pl.BlockSpec(memory_space=pltpu.VMEM)
    return pl.pallas_call(
        functools.partial(dispatch_kernel, 2 * blocks, capacity),
        out_shape=[jax.ShapeDtypeStruct((2 * capacity, width), BF16)] * blocks,
        in_specs=[pl.BlockSpec(memory_space=pltpu.SMEM), vmem, vmem],
        out_specs=[vmem] * blocks,
        compiler_params=pltpu.CompilerParams(vmem_limit_bytes=VMEM_LIMIT),
        cost_estimate=pl.CostEstimate(
            flops=4 * blocks * capacity * tokens.shape[0] * width,
            bytes_accessed=4 * blocks * capacity * width + 2 * tokens.size,
            transcendentals=0,
        ),
        name="dispatch",
    )(me, meta, tokens)


def mix_kernel(experts, capacity, blocks, has_extra, me_ref, meta_ref, *refs):
    parts = refs[:blocks]
    extra = refs[blocks] if has_extra else None
    out, held, sems = refs[-3], refs[-2], refs[-1]
    rows = parts[0].shape[0]
    copies = [
        pltpu.make_async_copy(part, held.at[pl.ds(k * rows, rows)], sems.at[k])
        for k, part in enumerate(parts)
    ]
    for copy in copies:
        copy.start()
    mask, weight = slot_masks(me_ref[0], meta_ref[...], experts, capacity)
    tokens = weight.shape[1]
    spread = jnp.where(mask, weight[:, None, :], 0.0).reshape(experts * capacity, tokens)
    high = spread.astype(BF16)
    low = (spread - high.astype(F32)).astype(BF16)
    for copy in copies:
        copy.wait()
    width = held.shape[1]
    tile = min(width, 512)
    over_slots = (((0,), (0,)), ((), ()))
    for col in range(0, width, tile):
        rows_here = held[:, col : col + tile]
        mixed = lax.dot_general(high, rows_here, over_slots, preferred_element_type=F32)
        mixed += lax.dot_general(low, rows_here, over_slots, preferred_element_type=F32)
        if extra is not None:
            mixed += extra[:, col : col + tile].astype(F32)
        out[:, col : col + tile] = mixed.astype(BF16)


def mix(me, meta, parts, capacity, extra=None):
    blocks = len(parts)
    rows, width = parts[0].shape
    tokens = meta.shape[1]
    vmem = pl.BlockSpec(memory_space=pltpu.VMEM)
    more = [] if extra is None else [extra]
    return pl.pallas_call(
        functools.partial(mix_kernel, 2 * blocks, capacity, blocks, bool(more)),
        out_shape=jax.ShapeDtypeStruct((tokens, width), BF16),
        in_specs=[pl.BlockSpec(memory_space=pltpu.SMEM), vmem]
        + [pl.BlockSpec(memory_space=pl.ANY)] * blocks
        + [vmem] * len(more),
        out_specs=vmem,
        scratch_shapes=[
            pltpu.VMEM((blocks * rows, width), BF16),
            pltpu.SemaphoreType.DMA((blocks,)),
        ],
        compiler_params=pltpu.CompilerParams(vmem_limit_bytes=VMEM_LIMIT),
        cost_estimate=pl.CostEstimate(
            flops=4 * blocks * rows * tokens * width,
            bytes_accessed=2 * blocks * rows * width + 4 * tokens * width,
            transcendentals=0,
        ),
        name="mix",
    )(me, meta, *parts, *more)


def experts_kernel(blocks, capacity, tiles, *refs):
    parts = refs[:blocks]
    gates, ups, downs = refs[blocks : blocks + 2], refs[blocks + 2 : blocks + 4], refs[blocks + 4 : blocks + 6]
    outs = refs[blocks + 6 : 2 * blocks + 6]
    rows_in, gate, up, down, hidden, part_sems, gate_sems, up_sems, down_sems = refs[2 * blocks + 6 :]
    units = gate.shape[2]
    width = down.shape[2]
    unit_tile, width_tile = units // tiles, width // tiles

    def part_copy(k, e):
        return pltpu.make_async_copy(
            parts[k].at[pl.ds(e * capacity, capacity)],
            rows_in.at[e, pl.ds(k * capacity, capacity)],
            part_sems.at[e, k],
        )

    def column_copy(source, target, sems, e, i, tile):
        columns = pl.ds(i * tile, tile)
        return pltpu.make_async_copy(
            source[e].at[0, :, columns], target.at[e, :, columns], sems.at[e, i]
        )

    for e in range(2):
        for k in range(blocks):
            part_copy(k, e).start()
        for i in range(tiles):
            column_copy(gates, gate, gate_sems, e, i, unit_tile).start()
            column_copy(ups, up, up_sems, e, i, unit_tile).start()
    for e in range(2):
        for i in range(tiles):
            column_copy(downs, down, down_sems, e, i, width_tile).start()
    for e in range(2):
        for k in range(blocks):
            part_copy(k, e).wait()
        for i in range(tiles):
            column_copy(gates, gate, gate_sems, e, i, unit_tile).wait()
            column_copy(ups, up, up_sems, e, i, unit_tile).wait()
            columns = slice(i * unit_tile, (i + 1) * unit_tile)
            x = rows_in[e]
            gate_value = jnp.dot(x, gate[e, :, columns], preferred_element_type=F32)
            up_value = jnp.dot(x, up[e, :, columns], preferred_element_type=F32)
            hidden[e, :, columns] = (jax.nn.silu(gate_value) * up_value).astype(BF16)
    for e in range(2):
        for i in range(tiles):
            column_copy(downs, down, down_sems, e, i, width_tile).wait()
            columns = slice(i * width_tile, (i + 1) * width_tile)
            result = jnp.dot(hidden[e], down[e, :, columns], preferred_element_type=F32)
            result = result.astype(BF16)
            for k, out in enumerate(outs):
                out[e * capacity : (e + 1) * capacity, columns] = result[
                    k * capacity : (k + 1) * capacity
                ]


def run_experts(parts, gates, ups, downs, capacity):
    blocks = len(parts)
    _, width, units = gates[0].shape
    rows = blocks * capacity
    tiles = 4
    anywhere = pl.BlockSpec(memory_space=pl.ANY)
    return pl.pallas_call(
        functools.partial(experts_kernel, blocks, capacity, tiles),
        out_shape=[jax.ShapeDtypeStruct((2 * capacity, width), BF16)] * blocks,
        in_specs=[anywhere] * (blocks + 6),
        out_specs=[pl.BlockSpec(memory_space=pltpu.VMEM)] * blocks,
        scratch_shapes=[
            pltpu.VMEM((2, rows, width), BF16),
            pltpu.VMEM((2, width, units), BF16),
            pltpu.VMEM((2, width, units), BF16),
            pltpu.VMEM((2, units, width), BF16),
            pltpu.VMEM((2, rows, units), BF16),
            pltpu.SemaphoreType.DMA((2, blocks)),
            pltpu.SemaphoreType.DMA((2, tiles)),
            pltpu.SemaphoreType.DMA((2, tiles)),
            pltpu.SemaphoreType.DMA((2, tiles)),
        ],
        compiler_params=pltpu.CompilerParams(vmem_limit_bytes=VMEM_LIMIT),
        cost_estimate=pl.CostEstimate(
            flops=12 * rows * width * units,
            bytes_accessed=12 * width * units + 8 * rows * width,
            transcendentals=2 * rows * units,
        ),
        name="experts",
    )(*parts, *gates, *ups, *downs)


def run_experts_split(parts, gates, ups, downs, capacity):
    blocks = len(parts)
    rows = jnp.stack(parts).reshape(blocks, 2, capacity, -1)
    rows = lax.all_gather(rows, "tensor", axis=3, tiled=True)
    width = rows.shape[3]
    partial = []
    for e in range(2):
        x = rows[:, e].reshape(blocks * capacity, width)
        gate_value = jnp.dot(x, gates[e][0], preferred_element_type=F32)
        up_value = jnp.dot(x, ups[e][0], preferred_element_type=F32)
        hidden = (jax.nn.silu(gate_value) * up_value).astype(BF16)
        result = jnp.dot(hidden, downs[e][0], preferred_element_type=F32)
        partial.append(result.reshape(blocks, capacity, width))
    partial = jnp.stack(partial, axis=1).astype(BF16)
    reduced = lax.psum_scatter(partial, "tensor", scatter_dimension=3, tiled=True)
    reduced = reduced.reshape(blocks, 2 * capacity, -1)
    return [reduced[k] for k in range(blocks)]


def body(tokens, expert_ids, route_weights, gate_weight, up_weight, down_weight):
    groups = lax.axis_size("dp")
    capacity = 4 * tokens.shape[0] // groups
    half = groups // 2
    blocks = half // 2
    me = lax.axis_index("dp").astype(jnp.int32).reshape(1)

    def swap(x, distance):
        return lax.ppermute(x, "dp", [(i, i ^ distance) for i in range(groups)])

    def spread(parts):
        return [parts[0]] + [swap(parts[k], 2 * k) for k in range(1, blocks)]

    meta = jnp.concatenate([expert_ids.T.astype(F32), route_weights.T], axis=0)
    far_tokens = swap(tokens, half)
    far_meta = swap(meta, half)
    gates = (gate_weight, swap(gate_weight, 1))
    ups = (up_weight, swap(up_weight, 1))
    downs = (down_weight, swap(down_weight, 1))
    run = run_experts if lax.axis_size("tensor") == 1 else run_experts_split

    near_rows = spread(dispatch(me, meta, tokens, blocks, capacity))
    far_rows = spread(dispatch(me, far_meta, far_tokens, blocks, capacity))
    near_results = run(near_rows, gates, ups, downs, capacity)
    far_results = run(far_rows, gates, ups, downs, capacity)
    far_sum = mix(me, far_meta, spread(far_results), capacity)
    far_sum, near_results = lax.optimization_barrier((far_sum, near_results))
    back = swap(far_sum, half)
    return mix(me, meta, spread(near_results), capacity, back)


def solution(mesh):
    return jax.shard_map(
        body,
        mesh=mesh,
        in_specs=(
            P("dp", "tensor"),
            P("dp", None),
            P("dp", None),
            P("dp", None, "tensor"),
            P("dp", None, "tensor"),
            P("dp", "tensor", None),
        ),
        out_specs=P("dp", "tensor"),
        check_vma=False,
    )
```

```python
import functools

import jax
import jax.numpy as jnp
from jax import lax
from jax.experimental import pallas as pl
from jax.experimental.pallas import tpu as pltpu
from jax.sharding import PartitionSpec as P


MIB = 1024 * 1024
F32 = jnp.float32
BF16 = jnp.bfloat16
CHUNKS = 2


def plan_kernel(experts, capacity, me_ref, ids_ref, weights_ref, pick_ref, high_ref, low_ref):
    ids, route = ids_ref[...], weights_ref[...]
    tokens = ids.shape[1]
    names = jnp.bitwise_xor(
        me_ref[0], lax.broadcasted_iota(jnp.int32, (experts, tokens), 0)
    ).astype(ids.dtype)
    first = ids[0:1, :] == names
    second = ids[1:2, :] == names
    named = jnp.where(first, 1.0, 0.0) + jnp.where(second, 1.0, 0.0)
    weight = jnp.where(first, route[0:1, :], 0.0) + jnp.where(second, route[1:2, :], 0.0)
    earlier = jnp.where(
        lax.broadcasted_iota(jnp.int32, (tokens, tokens), 0)
        < lax.broadcasted_iota(jnp.int32, (tokens, tokens), 1),
        1.0,
        0.0,
    )
    rank = jnp.dot(named.astype(BF16), earlier.astype(BF16), preferred_element_type=F32)
    rank = jnp.where(named > 0.5, rank, -1.0).astype(jnp.int32)
    slot = lax.broadcasted_iota(jnp.int32, (experts, capacity, tokens), 1)
    mask = rank[:, None, :] == slot
    slots = experts * capacity
    pick_ref[...] = jnp.where(mask, 1.0, 0.0).reshape(slots, tokens).astype(BF16)
    spread = jnp.where(mask, weight[:, None, :], 0.0).reshape(slots, tokens).T
    high = spread.astype(BF16)
    high_ref[...] = high
    low_ref[...] = (spread - high.astype(F32)).astype(BF16)


def make_plan(me, ids, route, blocks, capacity):
    tokens = ids.shape[1]
    slots = 2 * blocks * capacity
    vmem = pl.BlockSpec(memory_space=pltpu.VMEM)
    return pl.pallas_call(
        functools.partial(plan_kernel, 2 * blocks, capacity),
        out_shape=[
            jax.ShapeDtypeStruct((slots, tokens), BF16),
            jax.ShapeDtypeStruct((tokens, slots), BF16),
            jax.ShapeDtypeStruct((tokens, slots), BF16),
        ],
        in_specs=[pl.BlockSpec(memory_space=pltpu.SMEM), vmem, vmem],
        out_specs=[vmem] * 3,
        compiler_params=pltpu.CompilerParams(vmem_limit_bytes=6 * MIB),
        cost_estimate=pl.CostEstimate(
            flops=40 * slots * tokens, bytes_accessed=6 * slots * tokens, transcendentals=0
        ),
        name="plan",
    )(me, ids, route)


def dispatch_kernel(blocks, pick_ref, tokens_ref, *refs):
    outs, rest = refs[:blocks], refs[blocks:]
    width = tokens_ref.shape[1]
    rows = outs[0].shape[0]
    for i, copy in enumerate(rest):
        step = copy.shape[1]
        copy[...] = tokens_ref[:, i * step : (i + 1) * step]
    tile = min(width, 512)
    for col in range(0, width, tile):
        picked = jnp.dot(pick_ref[...], tokens_ref[:, col : col + tile], preferred_element_type=F32)
        picked = picked.astype(BF16)
        for k, out in enumerate(outs):
            out[:, col : col + tile] = picked[k * rows : (k + 1) * rows]


def dispatch(plan, tokens, blocks, rest=0):
    pick = plan[0]
    slots = pick.shape[0]
    width = tokens.shape[1]
    vmem = pl.BlockSpec(memory_space=pltpu.VMEM)
    return pl.pallas_call(
        functools.partial(dispatch_kernel, blocks),
        out_shape=[jax.ShapeDtypeStruct((slots // blocks, width), BF16)] * blocks
        + [jax.ShapeDtypeStruct((tokens.shape[0], width // max(rest, 1)), BF16)] * rest,
        in_specs=[vmem, vmem],
        out_specs=[vmem] * (blocks + rest),
        compiler_params=pltpu.CompilerParams(vmem_limit_bytes=8 * MIB),
        cost_estimate=pl.CostEstimate(
            flops=2 * slots * tokens.shape[0] * width,
            bytes_accessed=2 * slots * width + 2 * tokens.size,
            transcendentals=0,
        ),
        name="dispatch",
    )(pick, tokens)


def mix_kernel(blocks, high_ref, low_ref, *refs):
    parts = refs[:blocks]
    out, held, sems = refs[blocks:]
    rows = parts[0].shape[0]
    copies = [
        pltpu.make_async_copy(part, held.at[pl.ds(k * rows, rows)], sems.at[k])
        for k, part in enumerate(parts)
    ]
    for copy in copies:
        copy.start()
    for copy in copies:
        copy.wait()
    width = held.shape[1]
    tile = min(width, 512)
    for col in range(0, width, tile):
        rows_here = held[:, col : col + tile]
        mixed = jnp.dot(high_ref[...], rows_here, preferred_element_type=F32)
        mixed += jnp.dot(low_ref[...], rows_here, preferred_element_type=F32)
        out[:, col : col + tile] = mixed.astype(out.dtype)


def mix(plan, parts, dtype):
    blocks = len(parts)
    _, width = parts[0].shape
    _, high, low = plan
    tokens, slots = high.shape
    vmem = pl.BlockSpec(memory_space=pltpu.VMEM)
    return pl.pallas_call(
        functools.partial(mix_kernel, blocks),
        out_shape=jax.ShapeDtypeStruct((tokens, width), dtype),
        in_specs=[vmem, vmem] + [pl.BlockSpec(memory_space=pl.ANY)] * blocks,
        out_specs=vmem,
        scratch_shapes=[
            pltpu.VMEM((slots, width), BF16),
            pltpu.SemaphoreType.DMA((blocks,)),
        ],
        compiler_params=pltpu.CompilerParams(vmem_limit_bytes=8 * MIB),
        cost_estimate=pl.CostEstimate(
            flops=4 * slots * tokens * width,
            bytes_accessed=2 * slots * width + 4 * tokens * width,
            transcendentals=0,
        ),
        name="mix",
    )(high, low, *parts)


def experts_kernel(blocks, capacity, widths, first, *refs):
    pieces = blocks * len(widths)
    refs = list(refs)

    def take(n):
        taken = refs[:n]
        del refs[:n]
        return taken

    parts, gates, ups = take(pieces), take(2), take(2)
    downs = take(2) if first else None
    outs = take(blocks) if first else []
    hidden, rows_in, gate, up, part_sems, gate_sems, up_sems = take(7)
    down, down_sems = refs if first else (None, None)
    tile = gate.shape[2] // gate_sems.shape[1]
    down_tiles = down_sems.shape[1] if first else 0
    down_tile = first // max(down_tiles, 1)
    offsets = [sum(widths[:i]) for i in range(len(widths))]

    def part_copy(e, n):
        chunk, k = divmod(n, blocks)
        return pltpu.make_async_copy(
            parts[n].at[pl.ds(e * capacity, capacity)],
            rows_in.at[e, pl.ds(k * capacity, capacity), pl.ds(offsets[chunk], widths[chunk])],
            part_sems.at[e, n],
        )

    def weight_copy(source, target, sems, e, i, size):
        columns = pl.ds(i * size, size)
        return pltpu.make_async_copy(
            source[e].at[0, :, columns], target.at[e, :, columns], sems.at[e, i]
        )

    for e in range(2):
        for n in range(pieces):
            part_copy(e, n).start()
        for i in range(gate_sems.shape[1]):
            weight_copy(gates, gate, gate_sems, e, i, tile).start()
            weight_copy(ups, up, up_sems, e, i, tile).start()
    for e in range(2):
        for i in range(down_tiles):
            weight_copy(downs, down, down_sems, e, i, down_tile).start()
    for e in range(2):
        for n in range(pieces):
            part_copy(e, n).wait()
        for i in range(gate_sems.shape[1]):
            weight_copy(gates, gate, gate_sems, e, i, tile).wait()
            weight_copy(ups, up, up_sems, e, i, tile).wait()
            columns = slice(i * tile, (i + 1) * tile)
            x = rows_in[e]
            gate_value = jnp.dot(x, gate[e, :, columns], preferred_element_type=F32)
            up_value = jnp.dot(x, up[e, :, columns], preferred_element_type=F32)
            hidden[e, :, columns] = (jax.nn.silu(gate_value) * up_value).astype(BF16)
    for e in range(2):
        for i in range(down_tiles):
            weight_copy(downs, down, down_sems, e, i, down_tile).wait()
            columns = slice(i * down_tile, (i + 1) * down_tile)
            result = jnp.dot(hidden[e], down[e, :, columns], preferred_element_type=F32)
            result = result.astype(BF16)
            for k, out in enumerate(outs):
                out[e * capacity : (e + 1) * capacity, columns] = result[
                    k * capacity : (k + 1) * capacity
                ]


def run_hidden(chunks, gates, ups, downs, capacity, first):
    blocks = len(chunks[0])
    widths = tuple(chunk[0].shape[1] for chunk in chunks)
    _, width, units = gates[0].shape
    rows = blocks * capacity
    pieces = [part for chunk in chunks for part in chunk]
    tiles, down_tiles = 2, first // min(max(first, 1), 512)
    anywhere = pl.BlockSpec(memory_space=pl.ANY)
    vmem = pl.BlockSpec(memory_space=pltpu.VMEM)
    weights = [*gates, *ups] + (list(downs) if first else [])
    sent = blocks if first else 0
    scratch = [
        pltpu.VMEM((2, rows, width), BF16),
        pltpu.VMEM((2, width, units), BF16),
        pltpu.VMEM((2, width, units), BF16),
        pltpu.SemaphoreType.DMA((2, len(pieces))),
        pltpu.SemaphoreType.DMA((2, tiles)),
        pltpu.SemaphoreType.DMA((2, tiles)),
    ]
    if first:
        scratch += [
            pltpu.VMEM((2, units, first), BF16),
            pltpu.SemaphoreType.DMA((2, down_tiles)),
        ]
    return pl.pallas_call(
        functools.partial(experts_kernel, blocks, capacity, widths, first),
        out_shape=[jax.ShapeDtypeStruct((2 * capacity, first), BF16)] * sent
        + [jax.ShapeDtypeStruct((2, rows, units), BF16)],
        in_specs=[anywhere] * (len(pieces) + len(weights)),
        out_specs=[vmem] * (sent + 1),
        scratch_shapes=scratch,
        compiler_params=pltpu.CompilerParams(vmem_limit_bytes=46 * MIB),
        cost_estimate=pl.CostEstimate(
            flops=8 * rows * width * units + 4 * rows * first * units,
            bytes_accessed=8 * width * units + 4 * first * units + 8 * rows * width,
            transcendentals=2 * rows * units,
        ),
        name="experts",
    )(*pieces, *weights)


def down_kernel(blocks, capacity, start, tile, hidden, own, other, *refs):
    outs = refs[:blocks]
    down, sems = refs[blocks:]
    tiles = down.shape[2] // tile

    def copy(e, i):
        return pltpu.make_async_copy(
            (own, other)[e].at[0, :, pl.ds(start + i * tile, tile)],
            down.at[e, :, pl.ds(i * tile, tile)],
            sems.at[e, i],
        )

    for i in range(tiles):
        for e in range(2):
            copy(e, i).start()
    for i in range(tiles):
        for e in range(2):
            copy(e, i).wait()
            columns = slice(i * tile, (i + 1) * tile)
            result = jnp.dot(hidden[e], down[e, :, columns], preferred_element_type=F32)
            result = result.astype(BF16)
            for k, out in enumerate(outs):
                out[e * capacity : (e + 1) * capacity, columns] = result[
                    k * capacity : (k + 1) * capacity
                ]


def run_down(hidden, downs, start, width, blocks, capacity):
    _, rows, units = hidden.shape
    tile = min(width, 512)
    anywhere = pl.BlockSpec(memory_space=pl.ANY)
    vmem = pl.BlockSpec(memory_space=pltpu.VMEM)
    return pl.pallas_call(
        functools.partial(down_kernel, blocks, capacity, start, tile),
        out_shape=[jax.ShapeDtypeStruct((2 * capacity, width), BF16)] * blocks,
        in_specs=[vmem, anywhere, anywhere],
        out_specs=[vmem] * blocks,
        scratch_shapes=[
            pltpu.VMEM((2, units, width), BF16),
            pltpu.SemaphoreType.DMA((2, width // tile)),
        ],
        compiler_params=pltpu.CompilerParams(vmem_limit_bytes=20 * MIB),
        cost_estimate=pl.CostEstimate(
            flops=4 * rows * width * units,
            bytes_accessed=4 * width * units + 4 * rows * width + 4 * rows * units,
            transcendentals=0,
        ),
        name="down",
    )(hidden, *downs)


def run_near(rows, gates, ups, downs, capacity):
    width, blocks = rows[0].shape[1], len(rows)
    (hidden,) = run_hidden([rows], gates, ups, downs, capacity, 0)
    return run_down(hidden, downs, 0, width, blocks, capacity)


def run_far(chunks, gates, ups, downs, capacity):
    start, blocks = chunks[0][0].shape[1], len(chunks[0])
    *results, hidden = run_hidden(chunks, gates, ups, downs, capacity, start)
    results = [results]
    for chunk in chunks[1:]:
        width = chunk[0].shape[1]
        results.append(run_down(hidden, downs, start, width, blocks, capacity))
        start += width
    return results


def run_split(chunks, gates, ups, downs, capacity):
    blocks = len(chunks[0])
    rows = jnp.concatenate([jnp.stack(chunk) for chunk in chunks], axis=2)
    rows = rows.reshape(blocks, 2, capacity, -1)
    rows = lax.all_gather(rows, "tensor", axis=3, tiled=True)
    width = rows.shape[3]
    partial = []
    for e in range(2):
        x = rows[:, e].reshape(blocks * capacity, width)
        gate_value = jnp.dot(x, gates[e][0], preferred_element_type=F32)
        up_value = jnp.dot(x, ups[e][0], preferred_element_type=F32)
        hidden = (jax.nn.silu(gate_value) * up_value).astype(BF16)
        result = jnp.dot(hidden, downs[e][0], preferred_element_type=F32)
        partial.append(result.reshape(blocks, capacity, width))
    partial = jnp.stack(partial, axis=1).astype(BF16)
    reduced = lax.psum_scatter(partial, "tensor", scatter_dimension=3, tiled=True)
    reduced = reduced.reshape(blocks, 2 * capacity, -1)
    results, start = [], 0
    for chunk in chunks:
        stop = start + chunk[0].shape[1]
        results.append([reduced[k, :, start:stop] for k in range(blocks)])
        start = stop
    return results


def body(tokens, expert_ids, route_weights, gate_weight, up_weight, down_weight):
    groups = lax.axis_size("dp")
    count, _ = tokens.shape
    capacity = 4 * count // groups
    half = groups // 2
    blocks = half // 2
    me = lax.axis_index("dp").astype(jnp.int32).reshape(1)

    def swap(x, distance):
        return lax.ppermute(x, "dp", [(i, i ^ distance) for i in range(groups)])

    def spread(parts):
        order = sorted(range(1, blocks), key=lambda k: (-bin(k).count("1"), -k))
        moved = {k: swap(parts[k], 2 * k) for k in order}
        return [parts[0]] + [moved[k] for k in range(1, blocks)]

    whole = lax.axis_size("tensor") == 1

    ids, route = expert_ids.T, route_weights.T
    near_plan = make_plan(me, ids, route, blocks, capacity)
    picked = dispatch(near_plan, tokens, blocks, CHUNKS)
    far_tokens = []
    for i in range(CHUNKS):
        far_tokens.append(swap(picked[blocks + i], half))
    far_meta = swap(jnp.concatenate([ids.astype(F32), route], axis=0), half)
    near_rows = spread(picked[:blocks])
    gates = (gate_weight, swap(gate_weight, 1))
    ups = (up_weight, swap(up_weight, 1))
    downs = (down_weight, swap(down_weight, 1))
    far_plan = make_plan(me, far_meta[:2], far_meta[2:], blocks, capacity)
    far_rows = []
    for i in range(CHUNKS):
        far_parts = dispatch(far_plan, far_tokens[i], blocks)
        far_rows.append(spread(far_parts))
    if whole:
        near_results = run_near(near_rows, gates, ups, downs, capacity)
    else:
        near_results = run_split([near_rows], gates, ups, downs, capacity)[0]
    run = run_far if whole else run_split
    far_results = run(far_rows, gates, ups, downs, capacity)
    back = []
    for i in range(CHUNKS):
        returned = spread(far_results[i])
        mixed = mix(far_plan, returned, BF16)
        back.append(swap(mixed, half))
    returned = spread(near_results)
    near_sum = mix(near_plan, returned, F32)
    return (near_sum + jnp.concatenate(back, axis=1).astype(F32)).astype(BF16)


def solution(mesh):
    return jax.shard_map(
        body,
        mesh=mesh,
        in_specs=(
            P("dp", "tensor"),
            P("dp", None),
            P("dp", None),
            P("dp", None, "tensor"),
            P("dp", None, "tensor"),
            P("dp", "tensor", None),
        ),
        out_specs=P("dp", "tensor"),
        check_vma=False,
    )
```

```python
import functools

import jax
import jax.numpy as jnp
from jax import lax
from jax.experimental import pallas as pl
from jax.experimental.pallas import tpu as pltpu
from jax.sharding import PartitionSpec as P


MIB = 1024 * 1024
F32 = jnp.float32
BF16 = jnp.bfloat16
CHUNKS = 2


def plan_kernel(experts, capacity, me_ref, ids_ref, weights_ref, pick_ref, high_ref, low_ref):
    ids, route = ids_ref[...], weights_ref[...]
    tokens = ids.shape[1]
    names = jnp.bitwise_xor(
        me_ref[0], lax.broadcasted_iota(jnp.int32, (experts, tokens), 0)
    ).astype(ids.dtype)
    first = ids[0:1, :] == names
    second = ids[1:2, :] == names
    named = jnp.where(first, 1.0, 0.0) + jnp.where(second, 1.0, 0.0)
    weight = jnp.where(first, route[0:1, :], 0.0) + jnp.where(second, route[1:2, :], 0.0)
    earlier = jnp.where(
        lax.broadcasted_iota(jnp.int32, (tokens, tokens), 0)
        < lax.broadcasted_iota(jnp.int32, (tokens, tokens), 1),
        1.0,
        0.0,
    )
    rank = jnp.dot(named.astype(BF16), earlier.astype(BF16), preferred_element_type=F32)
    rank = jnp.where(named > 0.5, rank, -1.0).astype(jnp.int32)
    slot = lax.broadcasted_iota(jnp.int32, (experts, capacity, tokens), 1)
    mask = rank[:, None, :] == slot
    slots = experts * capacity
    pick_ref[...] = jnp.where(mask, 1.0, 0.0).reshape(slots, tokens).astype(BF16)
    spread = jnp.where(mask, weight[:, None, :], 0.0).reshape(slots, tokens).T
    high = spread.astype(BF16)
    high_ref[...] = high
    low_ref[...] = (spread - high.astype(F32)).astype(BF16)


def make_plan(me, ids, route, blocks, capacity):
    tokens = ids.shape[1]
    slots = 2 * blocks * capacity
    vmem = pl.BlockSpec(memory_space=pltpu.VMEM)
    return pl.pallas_call(
        functools.partial(plan_kernel, 2 * blocks, capacity),
        out_shape=[
            jax.ShapeDtypeStruct((slots, tokens), BF16),
            jax.ShapeDtypeStruct((tokens, slots), BF16),
            jax.ShapeDtypeStruct((tokens, slots), BF16),
        ],
        in_specs=[pl.BlockSpec(memory_space=pltpu.SMEM), vmem, vmem],
        out_specs=[vmem] * 3,
        compiler_params=pltpu.CompilerParams(vmem_limit_bytes=6 * MIB),
        cost_estimate=pl.CostEstimate(
            flops=40 * slots * tokens, bytes_accessed=6 * slots * tokens, transcendentals=0
        ),
        name="plan",
    )(me, ids, route)


def dispatch_kernel(blocks, pick_ref, tokens_ref, *refs):
    outs, rest = refs[:blocks], refs[blocks:]
    width = tokens_ref.shape[1]
    rows = outs[0].shape[0]
    for i, copy in enumerate(rest):
        step = copy.shape[1]
        copy[...] = tokens_ref[:, i * step : (i + 1) * step]
    tile = min(width, 512)
    for col in range(0, width, tile):
        picked = jnp.dot(pick_ref[...], tokens_ref[:, col : col + tile], preferred_element_type=F32)
        picked = picked.astype(BF16)
        for k, out in enumerate(outs):
            out[:, col : col + tile] = picked[k * rows : (k + 1) * rows]


def dispatch(plan, tokens, blocks, rest=0):
    pick = plan[0]
    slots = pick.shape[0]
    width = tokens.shape[1]
    vmem = pl.BlockSpec(memory_space=pltpu.VMEM)
    return pl.pallas_call(
        functools.partial(dispatch_kernel, blocks),
        out_shape=[jax.ShapeDtypeStruct((slots // blocks, width), BF16)] * blocks
        + [jax.ShapeDtypeStruct((tokens.shape[0], width // max(rest, 1)), BF16)] * rest,
        in_specs=[vmem, vmem],
        out_specs=[vmem] * (blocks + rest),
        compiler_params=pltpu.CompilerParams(vmem_limit_bytes=8 * MIB),
        cost_estimate=pl.CostEstimate(
            flops=2 * slots * tokens.shape[0] * width,
            bytes_accessed=2 * slots * width + 2 * tokens.size,
            transcendentals=0,
        ),
        name="dispatch",
    )(pick, tokens)


def mix_kernel(blocks, high_ref, low_ref, *refs):
    parts = refs[:blocks]
    out, held, sems = refs[blocks:]
    rows = parts[0].shape[0]
    copies = [
        pltpu.make_async_copy(part, held.at[pl.ds(k * rows, rows)], sems.at[k])
        for k, part in enumerate(parts)
    ]
    for copy in copies:
        copy.start()
    for copy in copies:
        copy.wait()
    width = held.shape[1]
    tile = min(width, 512)
    for col in range(0, width, tile):
        rows_here = held[:, col : col + tile]
        mixed = jnp.dot(high_ref[...], rows_here, preferred_element_type=F32)
        mixed += jnp.dot(low_ref[...], rows_here, preferred_element_type=F32)
        out[:, col : col + tile] = mixed.astype(out.dtype)


def mix(plan, parts, dtype):
    blocks = len(parts)
    _, width = parts[0].shape
    _, high, low = plan
    tokens, slots = high.shape
    vmem = pl.BlockSpec(memory_space=pltpu.VMEM)
    return pl.pallas_call(
        functools.partial(mix_kernel, blocks),
        out_shape=jax.ShapeDtypeStruct((tokens, width), dtype),
        in_specs=[vmem, vmem] + [pl.BlockSpec(memory_space=pl.ANY)] * blocks,
        out_specs=vmem,
        scratch_shapes=[
            pltpu.VMEM((slots, width), BF16),
            pltpu.SemaphoreType.DMA((blocks,)),
        ],
        compiler_params=pltpu.CompilerParams(vmem_limit_bytes=8 * MIB),
        cost_estimate=pl.CostEstimate(
            flops=4 * slots * tokens * width,
            bytes_accessed=2 * slots * width + 4 * tokens * width,
            transcendentals=0,
        ),
        name="mix",
    )(high, low, *parts)


def experts_kernel(blocks, capacity, widths, first, *refs):
    pieces = blocks * len(widths)
    refs = list(refs)

    def take(n):
        taken = refs[:n]
        del refs[:n]
        return taken

    parts, gates, ups = take(pieces), take(2), take(2)
    downs = take(2) if first else None
    outs = take(blocks) if first else []
    hidden, rows_in, gate, up, part_sems, gate_sems, up_sems = take(7)
    down, down_sems = refs if first else (None, None)
    tile = gate.shape[2] // gate_sems.shape[1]
    down_tiles = down_sems.shape[1] if first else 0
    down_tile = first // max(down_tiles, 1)
    offsets = [sum(widths[:i]) for i in range(len(widths))]

    def part_copy(e, n):
        chunk, k = divmod(n, blocks)
        return pltpu.make_async_copy(
            parts[n].at[pl.ds(e * capacity, capacity)],
            rows_in.at[e, pl.ds(k * capacity, capacity), pl.ds(offsets[chunk], widths[chunk])],
            part_sems.at[e, n],
        )

    def weight_copy(source, target, sems, e, i, size):
        columns = pl.ds(i * size, size)
        return pltpu.make_async_copy(
            source[e].at[0, :, columns], target.at[e, :, columns], sems.at[e, i]
        )

    for e in range(2):
        for n in range(pieces):
            part_copy(e, n).start()
        for i in range(gate_sems.shape[1]):
            weight_copy(gates, gate, gate_sems, e, i, tile).start()
            weight_copy(ups, up, up_sems, e, i, tile).start()
    for e in range(2):
        for i in range(down_tiles):
            weight_copy(downs, down, down_sems, e, i, down_tile).start()
    for e in range(2):
        for n in range(pieces):
            part_copy(e, n).wait()
        for i in range(gate_sems.shape[1]):
            weight_copy(gates, gate, gate_sems, e, i, tile).wait()
            weight_copy(ups, up, up_sems, e, i, tile).wait()
            columns = slice(i * tile, (i + 1) * tile)
            x = rows_in[e]
            gate_value = jnp.dot(x, gate[e, :, columns], preferred_element_type=F32)
            up_value = jnp.dot(x, up[e, :, columns], preferred_element_type=F32)
            hidden[e, :, columns] = (jax.nn.silu(gate_value) * up_value).astype(BF16)
    for e in range(2):
        for i in range(down_tiles):
            weight_copy(downs, down, down_sems, e, i, down_tile).wait()
            columns = slice(i * down_tile, (i + 1) * down_tile)
            result = jnp.dot(hidden[e], down[e, :, columns], preferred_element_type=F32)
            result = result.astype(BF16)
            for k, out in enumerate(outs):
                out[e * capacity : (e + 1) * capacity, columns] = result[
                    k * capacity : (k + 1) * capacity
                ]


def run_hidden(chunks, gates, ups, downs, capacity, first):
    blocks = len(chunks[0])
    widths = tuple(chunk[0].shape[1] for chunk in chunks)
    _, width, units = gates[0].shape
    rows = blocks * capacity
    pieces = [part for chunk in chunks for part in chunk]
    tiles, down_tiles = 2, first // min(max(first, 1), 512)
    anywhere = pl.BlockSpec(memory_space=pl.ANY)
    vmem = pl.BlockSpec(memory_space=pltpu.VMEM)
    weights = [*gates, *ups] + (list(downs) if first else [])
    sent = blocks if first else 0
    scratch = [
        pltpu.VMEM((2, rows, width), BF16),
        pltpu.VMEM((2, width, units), BF16),
        pltpu.VMEM((2, width, units), BF16),
        pltpu.SemaphoreType.DMA((2, len(pieces))),
        pltpu.SemaphoreType.DMA((2, tiles)),
        pltpu.SemaphoreType.DMA((2, tiles)),
    ]
    if first:
        scratch += [
            pltpu.VMEM((2, units, first), BF16),
            pltpu.SemaphoreType.DMA((2, down_tiles)),
        ]
    return pl.pallas_call(
        functools.partial(experts_kernel, blocks, capacity, widths, first),
        out_shape=[jax.ShapeDtypeStruct((2 * capacity, first), BF16)] * sent
        + [jax.ShapeDtypeStruct((2, rows, units), BF16)],
        in_specs=[anywhere] * (len(pieces) + len(weights)),
        out_specs=[vmem] * (sent + 1),
        scratch_shapes=scratch,
        compiler_params=pltpu.CompilerParams(vmem_limit_bytes=46 * MIB),
        cost_estimate=pl.CostEstimate(
            flops=8 * rows * width * units + 4 * rows * first * units,
            bytes_accessed=8 * width * units + 4 * first * units + 8 * rows * width,
            transcendentals=2 * rows * units,
        ),
        name="experts",
    )(*pieces, *weights)


def down_kernel(blocks, capacity, start, tile, hidden, own, other, *refs):
    outs = refs[:blocks]
    down, sems = refs[blocks:]
    tiles = down.shape[2] // tile

    def copy(e, i):
        return pltpu.make_async_copy(
            (own, other)[e].at[0, :, pl.ds(start + i * tile, tile)],
            down.at[e, :, pl.ds(i * tile, tile)],
            sems.at[e, i],
        )

    for i in range(tiles):
        for e in range(2):
            copy(e, i).start()
    for i in range(tiles):
        for e in range(2):
            copy(e, i).wait()
            columns = slice(i * tile, (i + 1) * tile)
            result = jnp.dot(hidden[e], down[e, :, columns], preferred_element_type=F32)
            result = result.astype(BF16)
            for k, out in enumerate(outs):
                out[e * capacity : (e + 1) * capacity, columns] = result[
                    k * capacity : (k + 1) * capacity
                ]


def run_down(hidden, downs, start, width, blocks, capacity):
    _, rows, units = hidden.shape
    tile = min(width, 512)
    anywhere = pl.BlockSpec(memory_space=pl.ANY)
    vmem = pl.BlockSpec(memory_space=pltpu.VMEM)
    return pl.pallas_call(
        functools.partial(down_kernel, blocks, capacity, start, tile),
        out_shape=[jax.ShapeDtypeStruct((2 * capacity, width), BF16)] * blocks,
        in_specs=[vmem, anywhere, anywhere],
        out_specs=[vmem] * blocks,
        scratch_shapes=[
            pltpu.VMEM((2, units, width), BF16),
            pltpu.SemaphoreType.DMA((2, width // tile)),
        ],
        compiler_params=pltpu.CompilerParams(vmem_limit_bytes=46 * MIB),
        cost_estimate=pl.CostEstimate(
            flops=4 * rows * width * units,
            bytes_accessed=4 * width * units + 4 * rows * width + 4 * rows * units,
            transcendentals=0,
        ),
        name="down",
    )(hidden, *downs)


def run_near(rows, gates, ups, downs, capacity):
    width, blocks = rows[0].shape[1], len(rows)
    (hidden,) = run_hidden([rows], gates, ups, downs, capacity, 0)
    return run_down(hidden, downs, 0, width, blocks, capacity)


def run_far(chunks, gates, ups, downs, capacity):
    start, blocks = chunks[0][0].shape[1], len(chunks[0])
    *results, hidden = run_hidden(chunks, gates, ups, downs, capacity, start)
    results = [results]
    for chunk in chunks[1:]:
        width = chunk[0].shape[1]
        results.append(run_down(hidden, downs, start, width, blocks, capacity))
        start += width
    return results


def run_split(chunks, gates, ups, downs, capacity):
    blocks = len(chunks[0])
    rows = jnp.concatenate([jnp.stack(chunk) for chunk in chunks], axis=2)
    rows = rows.reshape(blocks, 2, capacity, -1)
    rows = lax.all_gather(rows, "tensor", axis=3, tiled=True)
    width = rows.shape[3]
    partial = []
    for e in range(2):
        x = rows[:, e].reshape(blocks * capacity, width)
        gate_value = jnp.dot(x, gates[e][0], preferred_element_type=F32)
        up_value = jnp.dot(x, ups[e][0], preferred_element_type=F32)
        hidden = (jax.nn.silu(gate_value) * up_value).astype(BF16)
        result = jnp.dot(hidden, downs[e][0], preferred_element_type=F32)
        partial.append(result.reshape(blocks, capacity, width))
    partial = jnp.stack(partial, axis=1).astype(BF16)
    reduced = lax.psum_scatter(partial, "tensor", scatter_dimension=3, tiled=True)
    reduced = reduced.reshape(blocks, 2 * capacity, -1)
    results, start = [], 0
    for chunk in chunks:
        stop = start + chunk[0].shape[1]
        results.append([reduced[k, :, start:stop] for k in range(blocks)])
        start = stop
    return results


def body(tokens, expert_ids, route_weights, gate_weight, up_weight, down_weight):
    groups = lax.axis_size("dp")
    count, _ = tokens.shape
    capacity = 4 * count // groups
    half = groups // 2
    blocks = half // 2
    me = lax.axis_index("dp").astype(jnp.int32).reshape(1)

    def swap(x, distance):
        return lax.ppermute(x, "dp", [(i, i ^ distance) for i in range(groups)])

    def spread(parts):
        order = sorted(range(1, blocks), key=lambda k: (-bin(k).count("1"), -k))
        moved = {}
        for k in order:
            moved[k] = swap(parts[k], 2 * k)
        return [parts[0]] + [moved[k] for k in range(1, blocks)]

    whole = lax.axis_size("tensor") == 1

    ids, route = expert_ids.T, route_weights.T
    near_plan = make_plan(me, ids, route, blocks, capacity)
    picked = dispatch(near_plan, tokens, blocks, CHUNKS)
    far_tokens = []
    for i in range(CHUNKS):
        far_tokens.append(swap(picked[blocks + i], half))
    far_meta = swap(jnp.concatenate([ids.astype(F32), route], axis=0), half)
    near_rows = spread(picked[:blocks])
    stay = [
        pltpu.with_memory_space_constraint(w, pltpu.HBM) if whole else w
        for w in (gate_weight, up_weight, down_weight)
    ]
    gates = (stay[0], swap(gate_weight, 1))
    ups = (stay[1], swap(up_weight, 1))
    downs = (stay[2], swap(down_weight, 1))
    far_plan = make_plan(me, far_meta[:2], far_meta[2:], blocks, capacity)
    far_rows = []
    for i in range(CHUNKS):
        far_parts = dispatch(far_plan, far_tokens[i], blocks)
        far_rows.append(spread(far_parts))
    if whole:
        near_results = run_near(near_rows, gates, ups, downs, capacity)
    else:
        near_results = run_split([near_rows], gates, ups, downs, capacity)[0]
    run = run_far if whole else run_split
    far_results = run(far_rows, gates, ups, downs, capacity)
    back = []
    for i in range(CHUNKS):
        returned = spread(far_results[i])
        mixed = mix(far_plan, returned, BF16)
        back.append(swap(mixed, half))
    returned = spread(near_results)
    near_sum = mix(near_plan, returned, F32)
    return (near_sum + jnp.concatenate(back, axis=1).astype(F32)).astype(BF16)


def solution(mesh):
    return jax.shard_map(
        body,
        mesh=mesh,
        in_specs=(
            P("dp", "tensor"),
            P("dp", None),
            P("dp", None),
            P("dp", None, "tensor"),
            P("dp", None, "tensor"),
            P("dp", "tensor", None),
        ),
        out_specs=P("dp", "tensor"),
        check_vma=False,
    )
```
